512 devices in a mesh: doc: 32 (over y, x), seq: 16 (over z, core).
Axes of the slice: x: 4, y: 8, z: 8, core: 2. Of those that a mesh axis runs over, the one named last changes fastest.
Arguments:
- tokens: bfloat16 [131072, 1024], P(('doc', 'seq')), parts along dimension 0, may hold values from -8 to 8
- bottom_qkv: bfloat16 [1024, 3072], P('seq'), may hold values from -1 to 1
- bottom_out: bfloat16 [1024, 1024], P('seq'), may hold values from -0.5 to 0.5
- top_qkv: bfloat16 [1024, 3, 1024], P(None, None, 'seq'), may hold values from -1 to 1
- top_out: bfloat16 [1024, 1024], P('seq'), may hold values from -0.5 to 0.5
- cross_query: bfloat16 [1024, 1024], P('seq'), may hold values from -1 to 1
- cross_kv: bfloat16 [1024, 2, 1024], P(None, None, 'seq'), may hold values from -1 to 1
- cross_out: bfloat16 [1024, 1024], P('seq'), may hold values from -0.5 to 0.5
Outputs:
- encoded: bfloat16 [131072, 1024], P(('doc', 'seq')), parts along dimension 0
The draws below stay inside these ranges and needn't reach their ends.
There are 32 independent parts, one for each index of `doc`. The reference program is written for one: setup_inputs(seed, part) draws one part's arguments, and reference() takes and returns one part's arrays. A program takes and returns all parts, laid end to end along the dimension named above; an argument that names none is the same for every part. Nothing has to cross between parts.
All inputs are finite; a program needn't handle non-finite values.
Results may differ from the reference program's by a relative error of at most 0.013.
Values may be sent and summed in bfloat16 or wider, within the bound.
A program may use at most 64 MiB of HBM per device.

```python
import math
import jax
import jax.numpy as jnp
from jax import lax

D = 1024
H = 16
W = 512
POOL = 32
TOK_DEV = 256
TOKENS = 4096


def drawn_weight(key, shape):
    return jnp.clip(jax.random.normal(key, shape, jnp.float32), -6.0, 6.0) / math.sqrt(D)


def draw_tokens(key, part):
    gaussian = jax.random.normal(jax.random.fold_in(key, 7), (TOKENS, D), jnp.float32)
    return jnp.clip(gaussian, -6.0, 6.0).astype(jnp.bfloat16)


def draw_bottom_qkv(key, part):
    matrix = drawn_weight(jax.random.fold_in(key, 101), (D, 3 * D))
    return matrix.astype(jnp.bfloat16)


def draw_top_qkv(key, part):
    matrix = drawn_weight(jax.random.fold_in(key, 102), (D, 3, D))
    return matrix.astype(jnp.bfloat16)


def draw_cross_query(key, part):
    matrix = drawn_weight(jax.random.fold_in(key, 103), (D, D))
    return matrix.astype(jnp.bfloat16)


def draw_cross_kv(key, part):
    matrix = drawn_weight(jax.random.fold_in(key, 104), (D, 2, D))
    return matrix.astype(jnp.bfloat16)


def steps_of(own_key, extent, split, least, top_value):
    loudness, own = 1.0, jax.random.fold_in(own_key, 6)
    for dim, blocks in split:
        steps = jnp.exp(jax.random.uniform(jax.random.fold_in(own, dim), (blocks,), jnp.float32, least / len(split), top_value / len(split)))
        loudness = loudness * jnp.repeat(steps, extent[dim] // blocks).reshape([-1 if axis == dim else 1 for axis in range(len(extent))])
    return loudness


def centred(rng, shape, deviation, most, cuts=(), held_as=jnp.bfloat16):
    array = deviation * jax.random.normal(rng, shape, jnp.float32)
    if cuts:
        array = array * steps_of(rng, shape, cuts, -0.22, 0.18)
    return jnp.clip(array, -most, most).astype(held_as)


def setup_inputs(seed: int = 0, part: int = 0) -> dict:
    arg_keys = jax.random.split(jax.random.key(seed), 9)
    part_splits = jax.random.split(jax.random.fold_in(arg_keys[8], part), 9)
    tokens = draw_tokens(jax.random.fold_in(jax.random.fold_in(arg_keys[8], part), 71), part)
    bottom_qkv = draw_bottom_qkv(jax.random.fold_in(arg_keys[8], 71), part)
    bottom_out = centred(arg_keys[2], (D, D), (D // 8) ** -0.5, 0.5, ((0, 16),))
    top_qkv = draw_top_qkv(jax.random.fold_in(arg_keys[8], 71), part)
    top_out = centred(arg_keys[4], (D, D), (D // 8) ** -0.5, 0.5, ((0, 16),))
    cross_query = draw_cross_query(jax.random.fold_in(arg_keys[8], 71), part)
    cross_kv = draw_cross_kv(jax.random.fold_in(arg_keys[8], 71), part)
    cross_out = centred(arg_keys[7], (D, D), (D // 8) ** -0.5, 0.5, ((0, 16),))
    return dict(tokens=tokens, bottom_qkv=bottom_qkv, bottom_out=bottom_out, top_qkv=top_qkv, top_out=top_out, cross_query=cross_query, cross_kv=cross_kv, cross_out=cross_out)


EPS = 1e-06

def normed(values_in):
    values_in = values_in.astype(jnp.float32)
    return (values_in * lax.rsqrt(lax.optimization_barrier(jnp.mean(values_in * values_in, axis=-1, keepdims=True)) + EPS)).astype(jnp.bfloat16)

def window_mask(first_tok, tok_count, half_win, total_tok):
    query_pos = first_tok + jnp.arange(tok_count, dtype=jnp.int32)
    key_pos = first_tok - half_win + jnp.arange(tok_count + 2 * half_win, dtype=jnp.int32)
    offsets = key_pos[None, :] - query_pos[:, None]
    inside = (key_pos[None, :] >= 0) & (key_pos[None, :] < total_tok)
    return (offsets >= -half_win) & (offsets < half_win) & inside

def attend(queries, key_mat, value_mat, allowed, head_count):
    row_count = queries.shape[0]
    key_count = key_mat.shape[0]
    head_width = queries.shape[1] // head_count
    score_scale = 1.0 / math.sqrt(head_width)
    split_q = queries.reshape(row_count, head_count, head_width).transpose(1, 0, 2)
    split_k = key_mat.reshape(key_count, head_count, head_width).transpose(1, 0, 2)
    split_v = value_mat.reshape(key_count, head_count, head_width).transpose(1, 0, 2)

    def one_head(operands):
        query_h, key_h, value_h = operands
        scores = jnp.dot(query_h, key_h.T, preferred_element_type=jnp.float32) * score_scale
        if allowed is not None:
            scores = jnp.where(allowed, scores, -1e+30)
        row_peak = lax.optimization_barrier(jnp.max(scores, axis=1, keepdims=True))
        expo = jnp.exp(scores - row_peak)
        row_total = lax.optimization_barrier(jnp.sum(expo, axis=1, keepdims=True))
        mixture = jnp.dot(expo.astype(jnp.bfloat16), value_h, preferred_element_type=jnp.float32) / row_total
        return mixture.astype(jnp.bfloat16)
    merged = lax.map(one_head, (split_q, split_k, split_v))
    return merged.transpose(1, 0, 2).reshape(row_count, head_count * head_width)

def reference(tokens, bottom_qkv, bottom_out, top_qkv, top_out, cross_query, cross_kv, cross_out):
    token_count = tokens.shape[0]
    half_win = W // 2
    normed_tok = normed(tokens)
    project = jnp.dot(normed_tok, bottom_qkv, preferred_element_type=jnp.float32).astype(jnp.bfloat16)
    queries = project[:, :D]
    key_vals = project[:, D:]
    padded = jnp.pad(key_vals, ((half_win, half_win), (0, 0)))

    def block_attend(block):
        first_tok = block * TOK_DEV
        window_kv = lax.dynamic_slice_in_dim(padded, first_tok, TOK_DEV + 2 * half_win, 0)
        query_blk = lax.dynamic_slice_in_dim(queries, first_tok, TOK_DEV, 0)
        allowed = window_mask(first_tok, TOK_DEV, half_win, token_count)
        return attend(query_blk, window_kv[:, :D], window_kv[:, D:], allowed, H)
    attended = lax.map(block_attend, jnp.arange(token_count // TOK_DEV, dtype=jnp.int32)).reshape(token_count, D)
    lower_tok = (tokens.astype(jnp.float32) + jnp.dot(attended, bottom_out, preferred_element_type=jnp.float32)).astype(jnp.bfloat16)
    pooled = lax.optimization_barrier(jnp.mean(lower_tok.astype(jnp.float32).reshape(token_count // POOL, POOL, D), axis=1)).astype(jnp.bfloat16)
    unit_norm = normed(pooled)
    top_q = jnp.dot(unit_norm, top_qkv[:, 0, :], preferred_element_type=jnp.float32).astype(jnp.bfloat16)
    top_k = jnp.dot(unit_norm, top_qkv[:, 1, :], preferred_element_type=jnp.float32).astype(jnp.bfloat16)
    top_v = jnp.dot(unit_norm, top_qkv[:, 2, :], preferred_element_type=jnp.float32).astype(jnp.bfloat16)
    top_att = attend(top_q, top_k, top_v, None, H)
    top_units = (pooled.astype(jnp.float32) + jnp.dot(top_att, top_out, preferred_element_type=jnp.float32)).astype(jnp.bfloat16)
    upper_norm = normed(top_units)
    cross_keys = jnp.dot(upper_norm, cross_kv[:, 0, :], preferred_element_type=jnp.float32).astype(jnp.bfloat16)
    cross_vals = jnp.dot(upper_norm, cross_kv[:, 1, :], preferred_element_type=jnp.float32).astype(jnp.bfloat16)
    cross_q = jnp.dot(normed(lower_tok), cross_query, preferred_element_type=jnp.float32).astype(jnp.bfloat16)
    cross_att = attend(cross_q, cross_keys, cross_vals, None, H)
    cross_sum = jnp.dot(cross_att, cross_out, preferred_element_type=jnp.float32)
    return (lower_tok.astype(jnp.float32) + cross_sum).astype(jnp.bfloat16)
```

```python
import math

import jax
import jax.numpy as jnp
from jax import lax
from jax.experimental import pallas as pl
from jax.experimental.pallas import tpu as pltpu
from jax.sharding import PartitionSpec as P

POOL = 32
EPS = 1e-06
F32 = jnp.float32
BF16 = jnp.bfloat16
EXP_SCALE = math.log2(math.e) / 8.0
MESH = pl.DeviceIdType.MESH
BO, CQ, TO, CO = 0, 1, 2, 3
NEAREST = (1, 7, 2, 6, 3, 5, 4)


def nt(a, b):
    return lax.dot_general(a, b, (((1,), (1,)), ((), ())), preferred_element_type=F32)


def nn(a, b):
    return jnp.dot(a, b, preferred_element_type=F32)


def norm(v):
    return (v * lax.rsqrt(jnp.mean(v * v, axis=-1, keepdims=True) + EPS)).astype(BF16)


def kernel(
    tok, w_qkv, w_bo, w_cq, w_to, w_co, tqt, ckt, out,
    wq, w2, xr, acc, qb, kv, bias, at, lt, pooled, tat, ckv, cq,
    ring_s, ring_r, par_s, par_r, own_s, halo_s, halo_r, cast_s, cast_r, fwd_s, fwd_r,
):
    me = lax.axis_index("seq")
    z, c = me // 2, me % 2
    partner = 2 * z + 1 - c

    def same(r):
        return 2 * ((z + r) % 8) + c

    left, right = (me + 15) % 16, (me + 1) % 16
    far = (me + 16 + (2 * c - 1)) % 16

    def slot_of(p):
        d = (p + 8 - z) % 8
        up = d // 4
        return (1 - up) * 2 * d + up * (15 - 2 * d)

    def remote(src, dst, s, r, to):
        return pltpu.make_async_remote_copy(
            src_ref=src, dst_ref=dst, send_sem=s, recv_sem=r,
            device_id={"seq": to}, device_id_type=MESH,
        )

    barrier = pltpu.get_barrier_semaphore()
    for peer in [same(r) for r in range(1, 8)] + [partner, far]:
        pl.semaphore_signal(barrier, inc=1, device_id={"seq": peer}, device_id_type=MESH)
    pl.semaphore_wait(barrier, 9)

    own = [w_qkv, w_bo, w_cq, w_to, w_co]

    def full(w):
        return wq if w == 0 else w2.at[w - 1]

    def ring_copy(w, h, d):
        buf = full(w)
        now = 2 * h - 1 if d == 0 else 2 * h
        if h == 4:
            now = 7
        if h == 1:
            src = own[w]
        else:
            src = buf.at[2 * (now - 2 if h < 4 else (5 if d == 0 else 6)) + c]
        dst = buf.at[2 * now + c]
        if h == 4:
            src, dst = src.at[pl.ds(32 * d, 32)], dst.at[pl.ds(32 * d, 32)]
        k = 2 * (h - 1) + d
        return remote(src, dst, ring_s.at[w, k], ring_r.at[w, k], same(1 if d == 0 else 7))

    def par_copy(w, s):
        buf = full(w)
        src = own[w] if s == 0 else buf.at[2 * s + c]
        return remote(src, buf.at[2 * s + c], par_s.at[w, s], par_r.at[w, s], partner)

    def own_copy(w):
        return pltpu.make_async_copy(own[w], full(w).at[c], own_s.at[w])

    def launch(w):
        ring_copy(w, 1, 0).start()
        ring_copy(w, 1, 1).start()
        par_copy(w, 0).start()
        own_copy(w).start()

    def hop(w, h):
        for d in (0, 1):
            ring_copy(w, h, d).wait_recv()
            if h < 4:
                ring_copy(w, h + 1, d).start()
                par_copy(w, 2 * h - 1 + d).start()
        if h == 4:
            par_copy(w, 7).start()

    def settle(w):
        own_copy(w).wait()
        for s in range(8):
            par_copy(w, s).wait_recv()

    launch(0)

    xn = norm(tok[...].astype(F32))
    for p in range(8):
        xr[slot_of(p)] = xn[:, 128 * p : 128 * p + 128]

    row = lax.broadcasted_iota(jnp.int32, (128, 640), 0)
    col = lax.broadcasted_iota(jnp.int32, (128, 640), 1)
    for b in range(2):
        pos = me * 256 - 256 + 128 * b + col
        ok = (col >= row) & (col < row + 512) & (pos >= 0) & (pos < 4096)
        bias[b] = jnp.where(ok, 0.0, -1e30).astype(F32)

    def qkv_group(g):
        lhs = jnp.concatenate([xr[2 * g], xr[2 * g + 1]], axis=1)

        def tile(n, _):
            cols = pl.ds(pl.multiple_of(n * 512, 512), 512)
            part = nn(lhs, wq[4 * g : 4 * g + 4, :, cols].reshape(256, 512))
            acc[n] = part if g == 0 else acc[n] + part
            return 0

        lax.fori_loop(0, 6, tile, 0)

    hop(0, 1)
    own_copy(0).wait()
    par_copy(0, 0).wait_recv()
    par_copy(0, 1).wait_recv()
    qkv_group(0)
    hop(0, 2)
    par_copy(0, 2).wait_recv()
    par_copy(0, 3).wait_recv()
    qkv_group(1)
    hop(0, 3)
    par_copy(0, 4).wait_recv()
    par_copy(0, 5).wait_recv()
    qkv_group(2)
    hop(0, 4)
    par_copy(0, 6).wait_recv()
    par_copy(0, 7).wait_recv()
    qkv_group(3)

    for n in range(4):
        block = acc[2 + n].astype(BF16)
        for j in range(4):
            kv[(4 * n + j) % 8, n // 2, 256:512, :] = block[:, 128 * j : 128 * j + 128]

    def halo(p, side):
        dst = kv.at[p, :, pl.ds(512 - 512 * side, 256), :]
        return remote(
            kv.at[p, :, pl.ds(256, 256), :], dst,
            halo_s.at[p, side], halo_r.at[p, side], left if side == 0 else right,
        )

    for n in range(2):
        block = acc[n].astype(BF16)
        for j in range(4):
            qb[4 * n + j] = block[:, 128 * j : 128 * j + 128]
    for p in range(8):
        halo(p, 0).start()
        halo(p, 1).start()
    launch(1 + BO)
    launch(1 + CQ)

    events = {
        1: lambda: hop(1 + BO, 1), 2: lambda: hop(1 + CQ, 1),
        3: lambda: hop(1 + BO, 2), 4: lambda: hop(1 + CQ, 2),
        5: lambda: hop(1 + BO, 3), 6: lambda: hop(1 + CQ, 3),
        7: lambda: hop(1 + BO, 4),
    }

    def attention(p, _):
        halo(p, 0).wait_recv()
        halo(p, 1).wait_recv()
        slot = slot_of(p)
        even = lax.broadcasted_iota(jnp.int32, (128, 128), 1) < 64
        for b in range(2):
            q = qb[p, 128 * b : 128 * b + 128, :]
            zero = jnp.zeros_like(q)
            both = jnp.concatenate([jnp.where(even, q, zero), jnp.where(even, zero, q)], axis=0)
            s = nt(both, kv[p, 0, 128 * b : 128 * b + 640, :])
            s = (s.reshape(2, 128, 640) + bias[b][None]).reshape(256, 640)
            e = jnp.exp2((s - jnp.max(s, axis=1, keepdims=True)) * EXP_SCALE)
            total = jnp.sum(e, axis=1, keepdims=True)
            o = nn(e.astype(BF16), kv[p, 1, 128 * b : 128 * b + 640, :]) / total
            at[slot, 128 * b : 128 * b + 128, :] = jnp.where(even, o[:128], o[128:]).astype(BF16)
        for k, event in events.items():
            pl.when(p == k)(event)
        return 0

    lax.fori_loop(0, 8, attention, 0)
    launch(1 + TO)
    launch(1 + CO)

    def square(lhs8, w, put):
        lhs = jnp.concatenate([lhs8[s] for s in range(8)], axis=1)

        def tile(n, _):
            cols = pl.ds(pl.multiple_of(n * 256, 256), 256)
            put(n, cols, nn(lhs, w2[w, :, :, cols].reshape(1024, 256)))
            return 0

        lax.fori_loop(0, 4, tile, 0)

    settle(1 + BO)

    def put_lower(n, cols, o):
        lt[:, cols] = (tok[:, cols].astype(F32) + o).astype(BF16)

    square(at, BO, put_lower)

    def cast_copies(b, buf):
        mine = buf.at[me]
        sends = [remote(mine, mine, cast_s.at[b, 0], cast_r.at[b, 0], partner)]
        for r in range(1, 8):
            sends.append(remote(mine, mine, cast_s.at[b, r], cast_r.at[b, r], same(r)))
        return sends

    def fwd_copy(b, buf, r):
        there = buf.at[same(8 - r)]
        return remote(there, there, fwd_s.at[b, r], fwd_r.at[b, r], partner)

    def cast_start(b, buf):
        sends = cast_copies(b, buf)
        for r in (4, 3, 5, 2, 6, 1, 7, 0):
            sends[r].start()

    def cast_finish(b, buf):
        sends = cast_copies(b, buf)
        for r in NEAREST:
            sends[r].wait_recv()
            fwd_copy(b, buf, r).start()
        sends[0].wait_recv()
        for r in NEAREST:
            fwd_copy(b, buf, r).wait_recv()

    low = lt[...].astype(F32)
    pooled[me] = (jnp.sum(low.reshape(8, POOL, 1024), axis=1) * (1.0 / POOL)).astype(BF16).astype(F32)
    cast_start(0, pooled)
    hop(1 + CQ, 4)
    ln = norm(low)
    for p in range(8):
        xr[slot_of(p)] = ln[:, 128 * p : 128 * p + 128]
    hop(1 + TO, 1)
    cast_finish(0, pooled)

    un = norm(pooled[...].reshape(128, 1024))
    tq = nt(un, tqt[0]).astype(BF16)
    tk = nt(un, tqt[1]).astype(BF16)
    tvt = nt(tqt[2], un).astype(BF16)
    st = nt(tk, tq)
    e = jnp.exp2((st - jnp.max(st, axis=0, keepdims=True)) * EXP_SCALE)
    tat[me] = (nn(tvt, e.astype(BF16)) / jnp.sum(e, axis=0, keepdims=True)).astype(BF16)
    cast_start(1, tat)
    hop(1 + CO, 1)
    hop(1 + TO, 2)
    settle(1 + CQ)

    def put_query(n, cols, o):
        o = o.astype(BF16)
        cq[2 * n] = o[:, :128]
        cq[2 * n + 1] = o[:, 128:]

    square(xr, CQ, put_query)
    hop(1 + CO, 2)
    hop(1 + TO, 3)
    cast_finish(1, tat)
    hop(1 + CO, 3)
    hop(1 + TO, 4)
    settle(1 + TO)

    units = pooled[...].reshape(128, 1024)
    chips = []
    for s in range(8):
        off = (s + 1) // 2 * (1 - 2 * (s % 2))
        base = 2 * ((z + 8 + off) % 8)
        chips.append(tat[pl.ds(base, 2)].reshape(128, 128).T)
    ta = jnp.concatenate(chips, axis=1)
    units = units + nn(ta, w2[TO].reshape(1024, 1024))
    up = norm(units.astype(BF16).astype(F32))
    ckv[me, 0] = nt(ckt[0], up).astype(BF16)
    ckv[me, 1] = nt(ckt[1], up).astype(BF16)
    cast_start(2, ckv)
    hop(1 + CO, 4)
    settle(1 + CO)
    cast_finish(2, ckv)

    def cross(p, _):
        q = cq[p]
        even = lax.broadcasted_iota(jnp.int32, (256, 128), 1) < 64
        zero = jnp.zeros_like(q)
        both = jnp.concatenate([jnp.where(even, q, zero), jnp.where(even, zero, q)], axis=0)
        s = nn(both, ckv[pl.ds(2 * p, 2), 0].reshape(128, 128))
        e = jnp.exp2((s - jnp.max(s, axis=1, keepdims=True)) * EXP_SCALE)
        total = jnp.sum(e, axis=1, keepdims=True)
        o = nt(e.astype(BF16), ckv[pl.ds(2 * p, 2), 1].reshape(128, 128)) / total
        at[slot_of(p)] = jnp.where(even, o[:256], o[256:]).astype(BF16)
        return 0

    lax.fori_loop(0, 8, cross, 0)

    def put_out(n, cols, o):
        out[:, cols] = (lt[:, cols].astype(F32) + o).astype(BF16)

    square(at, CO, put_out)

    for w in range(5):
        for h in range(1, 5):
            ring_copy(w, h, 0).wait_send()
            ring_copy(w, h, 1).wait_send()
        for s in range(8):
            par_copy(w, s).wait_send()
    for p in range(8):
        halo(p, 0).wait_send()
        halo(p, 1).wait_send()
    for b, buf in enumerate((pooled, tat, ckv)):
        for copy in cast_copies(b, buf):
            copy.wait_send()
        for r in range(1, 8):
            fwd_copy(b, buf, r).wait_send()


def local(tokens, bottom_qkv, bottom_out, top_qkv, top_out, cross_query, cross_kv, cross_out):
    tqt = top_qkv.transpose(1, 2, 0)
    ckt = cross_kv.transpose(1, 2, 0)
    dma = pltpu.SemaphoreType.DMA
    return pl.pallas_call(
        kernel,
        out_shape=jax.ShapeDtypeStruct((256, 1024), BF16),
        in_specs=[pl.BlockSpec(memory_space=pltpu.VMEM)] * 8,
        out_specs=pl.BlockSpec(memory_space=pltpu.VMEM),
        scratch_shapes=[
            pltpu.VMEM((16, 64, 3072), BF16),
            pltpu.VMEM((4, 16, 64, 1024), BF16),
            pltpu.VMEM((8, 256, 128), BF16),
            pltpu.VMEM((6, 256, 512), F32),
            pltpu.VMEM((8, 256, 128), BF16),
            pltpu.VMEM((8, 2, 768, 128), BF16),
            pltpu.VMEM((2, 128, 640), F32),
            pltpu.VMEM((8, 256, 128), BF16),
            pltpu.VMEM((256, 1024), BF16),
            pltpu.VMEM((16, 8, 1024), F32),
            pltpu.VMEM((16, 64, 128), BF16),
            pltpu.VMEM((16, 2, 64, 128), BF16),
            pltpu.VMEM((8, 256, 128), BF16),
            dma((5, 8)), dma((5, 8)), dma((5, 8)), dma((5, 8)), dma((5,)),
            dma((8, 2)), dma((8, 2)),
            dma((3, 8)), dma((3, 8)), dma((3, 8)), dma((3, 8)),
        ],
        compiler_params=pltpu.CompilerParams(
            collective_id=0, has_side_effects=True, vmem_limit_bytes=60 * 1024 * 1024
        ),
        name="layer",
    )(tokens, bottom_qkv, bottom_out, cross_query, top_out, cross_out, tqt, ckt)


def solution(mesh):
    in_specs = (
        P(("doc", "seq"), None),
        P("seq", None),
        P("seq", None),
        P(None, None, "seq"),
        P("seq", None),
        P("seq", None),
        P(None, None, "seq"),
        P("seq", None),
    )
    out_specs = P(("doc", "seq"), None)
    return jax.shard_map(local, mesh=mesh, in_specs=in_specs, out_specs=out_specs, check_vma=False)
```

```python
import math

import jax
import jax.numpy as jnp
from jax import lax
from jax.experimental import pallas as pl
from jax.experimental.pallas import tpu as pltpu
from jax.sharding import PartitionSpec as P

POOL = 32
EPS = 1e-06
F32 = jnp.float32
BF16 = jnp.bfloat16
EXP_SCALE = math.log2(math.e) / 8.0
MESH = pl.DeviceIdType.MESH
BO, CQ, TO, CO = 0, 1, 2, 3
NEAREST = (1, 7, 2, 6, 3, 5, 4)


def nt(a, b):
    return lax.dot_general(a, b, (((1,), (1,)), ((), ())), preferred_element_type=F32)


def nn(a, b):
    return jnp.dot(a, b, preferred_element_type=F32)


def norm(v):
    return (v * lax.rsqrt(jnp.mean(v * v, axis=-1, keepdims=True) + EPS)).astype(BF16)


def kernel(
    tok, w_qkv, w_bo, w_cq, w_to, w_co, tqt, ckt, out,
    wq, w2, xr, acc, qb, kv, bias, at, lt, pooled, tat, ckv, cq, tokh, xh, acch,
    ring_s, ring_r, par_s, par_r, own_s, halo_s, halo_r, cast_s, cast_r, fwd_s, fwd_r,
    side_s, side_r, tok_s, tok_r,
):
    me = lax.axis_index("seq")
    z, c = me // 2, me % 2
    partner = 2 * z + 1 - c

    def same(r):
        return 2 * ((z + r) % 8) + c

    doc = lax.axis_index("doc")
    x, y = doc % 4, doc // 4
    half = (x + y) % 2
    across = (4 * y + x + 1 - 2 * (x % 2), 4 * (y + 1 - 2 * (y % 2)) + x)
    far = (me + 16 + (2 * c - 1)) % 16

    def slot_of(p):
        d = (p + 8 - z) % 8
        up = d // 4
        return (1 - up) * 2 * d + up * (15 - 2 * d)

    def remote(src, dst, s, r, to):
        return pltpu.make_async_remote_copy(
            src_ref=src, dst_ref=dst, send_sem=s, recv_sem=r,
            device_id={"seq": to}, device_id_type=MESH,
        )

    barrier = pltpu.get_barrier_semaphore()
    for peer in [same(r) for r in range(1, 8)] + [partner, far]:
        pl.semaphore_signal(barrier, inc=1, device_id={"seq": peer}, device_id_type=MESH)
    for peer in across:
        pl.semaphore_signal(barrier, inc=1, device_id={"doc": peer}, device_id_type=MESH)
    pl.semaphore_wait(barrier, 11)

    own = [w_qkv, w_bo, w_cq, w_to, w_co]

    def full(w):
        return wq if w == 0 else w2.at[w - 1]

    def arriving(h, d):
        return 7 if h == 4 else 2 * h - 1 + d

    def rows(buf, start):
        return buf.at[pl.ds(pl.multiple_of(start, 16), 16)]

    def ring_copy(w, h, d, i):
        buf = full(w)
        src = own[w] if h == 1 else buf.at[2 * arriving(h - 1, d) + c]
        dst = buf.at[2 * arriving(h, d) + c]
        at_row = 32 * half + 16 * i
        k = 4 * (h - 1) + 2 * d + i
        return remote(
            rows(src, at_row), rows(dst, at_row), ring_s.at[w, k], ring_r.at[w, k],
            same(1 if d == 0 else 7),
        )

    def side_copy(w, s, i):
        there = rows(full(w).at[2 * s + c], 32 * half + 16 * i)
        return pltpu.make_async_remote_copy(
            src_ref=there, dst_ref=there, send_sem=side_s.at[w, 2 * s + i],
            recv_sem=side_r.at[w, 2 * s + i],
            device_id={"doc": across[i]}, device_id_type=MESH,
        )

    def par_copy(w, s, j):
        if s == 0:
            src, dst = own[w], full(w).at[c]
        else:
            at_row = 32 * half + 16 * j if j < 2 else 32 * (1 - half) + 16 * (j - 2)
            src = dst = rows(full(w).at[2 * s + c], at_row)
        return remote(src, dst, par_s.at[w, 4 * s + j], par_r.at[w, 4 * s + j], partner)

    def own_copy(w):
        return pltpu.make_async_copy(own[w], full(w).at[c], own_s.at[w])

    def chunks(h):
        return [(d, i) for i in (0, 1) for d in (0, 1) if h < 4 or i == d]

    def launch(w):
        for d, i in chunks(1):
            ring_copy(w, 1, d, i).start()
        par_copy(w, 0, 0).start()
        own_copy(w).start()

    def hop(w, h):
        for d, i in chunks(h):
            ring_copy(w, h, d, i).wait_recv()
            if h < 4 and (d, i) in chunks(h + 1):
                ring_copy(w, h + 1, d, i).start()
            side_copy(w, arriving(h, d), i).start()
            par_copy(w, arriving(h, d), i).start()

    def lag(w, h):
        for d, i in chunks(h):
            side_copy(w, arriving(h, d), i).wait_recv()
            par_copy(w, arriving(h, d), 2 + i).start()

    def have(w, s):
        if s == 0:
            own_copy(w).wait()
            par_copy(w, 0, 0).wait_recv()
        else:
            for j in range(4):
                par_copy(w, s, j).wait_recv()

    def settle(w):
        for s in range(8):
            have(w, s)

    launch(0)
    tok_copy = remote(tok, tokh, tok_s, tok_r, far)
    tok_copy.start()

    xn = norm(tok[...].astype(F32))
    for p in range(8):
        xr[slot_of(p)] = xn[:, 128 * p : 128 * p + 128]

    row = lax.broadcasted_iota(jnp.int32, (128, 640), 0)
    col = lax.broadcasted_iota(jnp.int32, (128, 640), 1)
    for b in range(2):
        pos = me * 256 - 256 + 128 * b + col
        ok = (col >= row) & (col < row + 512) & (pos >= 0) & (pos < 4096)
        bias[b] = jnp.where(ok, 0.0, -1e30).astype(F32)

    def qkv_group(g):
        mine = jnp.concatenate([xr[2 * g], xr[2 * g + 1]], axis=1)
        both = jnp.concatenate(
            [mine, jnp.concatenate([xh[2 * g], xh[2 * g + 1]], axis=1)], axis=0
        )

        def tile_q(n, _):
            cols = pl.ds(pl.multiple_of(n * 512, 512), 512)
            part = nn(mine, wq[4 * g : 4 * g + 4, :, cols].reshape(256, 512))
            acc[n] = part if g == 0 else acc[n] + part
            return 0

        def tile_kv(n, _):
            cols = pl.ds(pl.multiple_of(1024 + n * 512, 512), 512)
            part = nn(both, wq[4 * g : 4 * g + 4, :, cols].reshape(256, 512))
            acch[n] = part if g == 0 else acch[n] + part
            return 0

        lax.fori_loop(0, 4, tile_kv, 0)
        lax.fori_loop(0, 2, tile_q, 0)

    hop(0, 1)
    hop(0, 2)
    lag(0, 1)
    tok_copy.wait_recv()
    xn = norm(tokh[...].astype(F32))
    for p in range(8):
        xh[slot_of(p)] = xn[:, 128 * p : 128 * p + 128]
    have(0, 0)
    have(0, 1)
    qkv_group(0)
    hop(0, 3)
    lag(0, 2)
    have(0, 2)
    have(0, 3)
    qkv_group(1)
    hop(0, 4)
    launch(1 + BO)
    launch(1 + CQ)
    lag(0, 3)
    have(0, 4)
    have(0, 5)
    qkv_group(2)
    lag(0, 4)
    have(0, 6)
    have(0, 7)
    qkv_group(3)

    far_rows = pl.ds(pl.multiple_of(512 * c, 256), 256)
    for n in range(4):
        block = acch[n].astype(BF16)
        for j in range(4):
            kv[(4 * n + j) % 8, n // 2, 256:512, :] = block[:256, 128 * j : 128 * j + 128]
            kv[(4 * n + j) % 8, n // 2, far_rows, :] = block[256:, 128 * j : 128 * j + 128]

    def halo(p):
        return remote(
            kv.at[p, :, pl.ds(256, 256), :], kv.at[p, :, far_rows, :],
            halo_s.at[p], halo_r.at[p], partner,
        )

    for n in range(2):
        block = acc[n].astype(BF16)
        for j in range(4):
            qb[4 * n + j] = block[:, 128 * j : 128 * j + 128]
    for p in range(8):
        halo(p).start()

    def event(*steps):
        def run():
            for step, w, *h in steps:
                step(1 + w, *h)
        return run

    events = {
        0: event((hop, BO, 1)), 1: event((hop, CQ, 1)),
        2: event((hop, BO, 2), (lag, BO, 1)), 3: event((hop, CQ, 2), (lag, CQ, 1)),
        4: event((hop, BO, 3), (lag, BO, 2)), 5: event((hop, CQ, 3), (lag, CQ, 2)),
        6: event((hop, BO, 4), (lag, BO, 3), (hop, CQ, 4), (lag, CQ, 3), (launch, TO), (launch, CO)),
        7: event((lag, BO, 4), (lag, CQ, 4)),
    }

    def attention(p, _):
        halo(p).wait_recv()
        slot = slot_of(p)
        even = lax.broadcasted_iota(jnp.int32, (128, 128), 1) < 64
        for b in range(2):
            q = qb[p, 128 * b : 128 * b + 128, :]
            zero = jnp.zeros_like(q)
            both = jnp.concatenate([jnp.where(even, q, zero), jnp.where(even, zero, q)], axis=0)
            s = nt(both, kv[p, 0, 128 * b : 128 * b + 640, :])
            s = (s.reshape(2, 128, 640) + bias[b][None]).reshape(256, 640)
            e = jnp.exp2((s - jnp.max(s, axis=1, keepdims=True)) * EXP_SCALE)
            total = jnp.sum(e, axis=1, keepdims=True)
            o = nn(e.astype(BF16), kv[p, 1, 128 * b : 128 * b + 640, :]) / total
            at[slot, 128 * b : 128 * b + 128, :] = jnp.where(even, o[:128], o[128:]).astype(BF16)
        for k, event in events.items():
            pl.when(p == k)(event)
        return 0

    lax.fori_loop(0, 8, attention, 0)

    def square(lhs8, w, put):
        lhs = jnp.concatenate([lhs8[s] for s in range(8)], axis=1)

        def tile(n, _):
            cols = pl.ds(pl.multiple_of(n * 256, 256), 256)
            put(n, cols, nn(lhs, w2[w, :, :, cols].reshape(1024, 256)))
            return 0

        lax.fori_loop(0, 4, tile, 0)

    settle(1 + BO)

    def put_lower(n, cols, o):
        lt[:, cols] = (tok[:, cols].astype(F32) + o).astype(BF16)

    square(at, BO, put_lower)

    def cast_copies(b, buf):
        mine = buf.at[me]
        sends = [remote(mine, mine, cast_s.at[b, 0], cast_r.at[b, 0], partner)]
        for r in range(1, 8):
            sends.append(remote(mine, mine, cast_s.at[b, r], cast_r.at[b, r], same(r)))
        return sends

    def fwd_copy(b, buf, r):
        there = buf.at[same(8 - r)]
        return remote(there, there, fwd_s.at[b, r], fwd_r.at[b, r], partner)

    def cast_start(b, buf):
        sends = cast_copies(b, buf)
        for r in (4, 3, 5, 2, 6, 1, 7, 0):
            sends[r].start()

    def cast_finish(b, buf):
        sends = cast_copies(b, buf)
        for r in NEAREST:
            sends[r].wait_recv()
            fwd_copy(b, buf, r).start()
        sends[0].wait_recv()
        for r in NEAREST:
            fwd_copy(b, buf, r).wait_recv()

    low = lt[...].astype(F32)
    pooled[me] = (jnp.sum(low.reshape(8, POOL, 1024), axis=1) * (1.0 / POOL)).astype(BF16).astype(F32)
    cast_start(0, pooled)
    ln = norm(low)
    for p in range(8):
        xr[slot_of(p)] = ln[:, 128 * p : 128 * p + 128]
    hop(1 + TO, 1)
    cast_finish(0, pooled)

    un = norm(pooled[...].reshape(128, 1024))
    tq = nt(un, tqt[0]).astype(BF16)
    tk = nt(un, tqt[1]).astype(BF16)
    tvt = nt(tqt[2], un).astype(BF16)
    st = nt(tk, tq)
    e = jnp.exp2((st - jnp.max(st, axis=0, keepdims=True)) * EXP_SCALE)
    tat[me] = (nn(tvt, e.astype(BF16)) / jnp.sum(e, axis=0, keepdims=True)).astype(BF16)
    cast_start(1, tat)
    hop(1 + CO, 1)
    hop(1 + TO, 2)
    lag(1 + TO, 1)
    settle(1 + CQ)

    def put_query(n, cols, o):
        o = o.astype(BF16)
        cq[2 * n] = o[:, :128]
        cq[2 * n + 1] = o[:, 128:]

    square(xr, CQ, put_query)
    hop(1 + TO, 3)
    lag(1 + TO, 2)
    hop(1 + CO, 2)
    lag(1 + CO, 1)
    hop(1 + TO, 4)
    lag(1 + TO, 3)
    cast_finish(1, tat)
    hop(1 + CO, 3)
    lag(1 + CO, 2)
    lag(1 + TO, 4)
    settle(1 + TO)

    units = pooled[...].reshape(128, 1024)
    chips = []
    for s in range(8):
        off = (s + 1) // 2 * (1 - 2 * (s % 2))
        base = 2 * ((z + 8 + off) % 8)
        chips.append(tat[pl.ds(base, 2)].reshape(128, 128).T)
    ta = jnp.concatenate(chips, axis=1)
    units = units + nn(ta, w2[TO].reshape(1024, 1024))
    up = norm(units.astype(BF16).astype(F32))
    ckv[me, 0] = nt(ckt[0], up).astype(BF16)
    ckv[me, 1] = nt(ckt[1], up).astype(BF16)
    cast_start(2, ckv)
    hop(1 + CO, 4)
    lag(1 + CO, 3)
    lag(1 + CO, 4)
    cast_finish(2, ckv)

    def cross(p, _):
        q = cq[p]
        even = lax.broadcasted_iota(jnp.int32, (256, 128), 1) < 64
        zero = jnp.zeros_like(q)
        both = jnp.concatenate([jnp.where(even, q, zero), jnp.where(even, zero, q)], axis=0)
        s = nn(both, ckv[pl.ds(2 * p, 2), 0].reshape(128, 128))
        e = jnp.exp2((s - jnp.max(s, axis=1, keepdims=True)) * EXP_SCALE)
        total = jnp.sum(e, axis=1, keepdims=True)
        o = nt(e.astype(BF16), ckv[pl.ds(2 * p, 2), 1].reshape(128, 128)) / total
        at[slot_of(p)] = jnp.where(even, o[:256], o[256:]).astype(BF16)
        return 0

    lax.fori_loop(0, 8, cross, 0)

    settle(1 + CO)

    def put_out(n, cols, o):
        out[:, cols] = (lt[:, cols].astype(F32) + o).astype(BF16)

    square(at, CO, put_out)

    for w in range(5):
        par_copy(w, 0, 0).wait_send()
        for h in range(1, 5):
            for d, i in chunks(h):
                ring_copy(w, h, d, i).wait_send()
                side_copy(w, arriving(h, d), i).wait_send()
                par_copy(w, arriving(h, d), i).wait_send()
                par_copy(w, arriving(h, d), 2 + i).wait_send()
    tok_copy.wait_send()
    for p in range(8):
        halo(p).wait_send()
    for b, buf in enumerate((pooled, tat, ckv)):
        for copy in cast_copies(b, buf):
            copy.wait_send()
        for r in range(1, 8):
            fwd_copy(b, buf, r).wait_send()


def local(tokens, bottom_qkv, bottom_out, top_qkv, top_out, cross_query, cross_kv, cross_out):
    tqt = top_qkv.transpose(1, 2, 0)
    ckt = cross_kv.transpose(1, 2, 0)
    dma = pltpu.SemaphoreType.DMA
    return pl.pallas_call(
        kernel,
        out_shape=jax.ShapeDtypeStruct((256, 1024), BF16),
        in_specs=[pl.BlockSpec(memory_space=pltpu.VMEM)] * 8,
        out_specs=pl.BlockSpec(memory_space=pltpu.VMEM),
        scratch_shapes=[
            pltpu.VMEM((16, 64, 3072), BF16),
            pltpu.VMEM((4, 16, 64, 1024), BF16),
            pltpu.VMEM((8, 256, 128), BF16),
            pltpu.VMEM((2, 256, 512), F32),
            pltpu.VMEM((8, 256, 128), BF16),
            pltpu.VMEM((8, 2, 768, 128), BF16),
            pltpu.VMEM((2, 128, 640), F32),
            pltpu.VMEM((8, 256, 128), BF16),
            pltpu.VMEM((256, 1024), BF16),
            pltpu.VMEM((16, 8, 1024), F32),
            pltpu.VMEM((16, 64, 128), BF16),
            pltpu.VMEM((16, 2, 64, 128), BF16),
            pltpu.VMEM((8, 256, 128), BF16),
            pltpu.VMEM((256, 1024), BF16),
            pltpu.VMEM((8, 256, 128), BF16),
            pltpu.VMEM((4, 512, 512), F32),
            dma((5, 16)), dma((5, 16)), dma((5, 32)), dma((5, 32)), dma((5,)),
            dma((8,)), dma((8,)),
            dma((3, 8)), dma((3, 8)), dma((3, 8)), dma((3, 8)),
            dma((5, 16)), dma((5, 16)), dma, dma,
        ],
        compiler_params=pltpu.CompilerParams(
            collective_id=0, has_side_effects=True, vmem_limit_bytes=60 * 1024 * 1024
        ),
        name="layer",
    )(tokens, bottom_qkv, bottom_out, cross_query, top_out, cross_out, tqt, ckt)


def solution(mesh):
    in_specs = (
        P(("doc", "seq"), None),
        P("seq", None),
        P("seq", None),
        P(None, None, "seq"),
        P("seq", None),
        P("seq", None),
        P(None, None, "seq"),
        P("seq", None),
    )
    out_specs = P(("doc", "seq"), None)
    return jax.shard_map(local, mesh=mesh, in_specs=in_specs, out_specs=out_specs, check_vma=False)
```

```python
import math

import jax
import jax.numpy as jnp
from jax import lax
from jax.experimental import pallas as pl
from jax.experimental.pallas import tpu as pltpu
from jax.sharding import PartitionSpec as P

POOL = 32
EPS = 1e-06
F32 = jnp.float32
BF16 = jnp.bfloat16
EXP_SCALE = math.log2(math.e) / 8.0
MESH = pl.DeviceIdType.MESH
BO, CQ, TO, CO = 0, 1, 2, 3
NEAREST = (1, 7, 2, 6, 3, 5, 4)


def nt(a, b):
    return lax.dot_general(a, b, (((1,), (1,)), ((), ())), preferred_element_type=F32)


def nn(a, b):
    return jnp.dot(a, b, preferred_element_type=F32)


def norm(v):
    return (v * lax.rsqrt(jnp.mean(v * v, axis=-1, keepdims=True) + EPS)).astype(BF16)


def kernel(
    tok, w_qkv, w_bo, w_cq, w_to, w_co, tq_hbm, ck_hbm, out,
    wq, w2, xr, acc, qb, kv, bias, at, lt, pooled, tat, ckv, cq, tokh, xh, acch,
    ring_s, ring_r, par_s, par_r, own_s, halo_s, halo_r, cast_s, cast_r, fwd_s, fwd_r,
    side_s, side_r, tok_s, tok_r, tqt, ckt, unit_s,
):
    me = lax.axis_index("seq")
    z, c = me // 2, me % 2
    partner = 2 * z + 1 - c

    def same(r):
        return 2 * ((z + r) % 8) + c

    doc = lax.axis_index("doc")
    x, y = doc % 4, doc // 4
    half = (x + y) % 2
    across = (4 * y + x + 1 - 2 * (x % 2), 4 * (y + 1 - 2 * (y % 2)) + x)
    far = (me + 16 + (2 * c - 1)) % 16

    def slot_of(p):
        d = (p + 8 - z) % 8
        up = d // 4
        return (1 - up) * 2 * d + up * (15 - 2 * d)

    def remote(src, dst, s, r, to):
        return pltpu.make_async_remote_copy(
            src_ref=src, dst_ref=dst, send_sem=s, recv_sem=r,
            device_id={"seq": to}, device_id_type=MESH,
        )

    unit_copies = (
        pltpu.make_async_copy(tq_hbm, tqt, unit_s.at[0]),
        pltpu.make_async_copy(ck_hbm, ckt, unit_s.at[1]),
    )
    for copy in unit_copies:
        copy.start()
    barrier = pltpu.get_barrier_semaphore()
    for peer in [same(r) for r in range(1, 8)] + [partner, far]:
        pl.semaphore_signal(barrier, inc=1, device_id={"seq": peer}, device_id_type=MESH)
    for peer in across:
        pl.semaphore_signal(barrier, inc=1, device_id={"doc": peer}, device_id_type=MESH)
    pl.semaphore_wait(barrier, 11)

    own = [w_qkv, w_bo, w_cq, w_to, w_co]

    def full(w):
        return wq if w == 0 else w2.at[w - 1]

    def arriving(h, d):
        return 7 if h == 4 else 2 * h - 1 + d

    def rows(buf, start):
        return buf.at[pl.ds(pl.multiple_of(start, 16), 16)]

    def ring_copy(w, h, d, i):
        buf = full(w)
        src = own[w] if h == 1 else buf.at[2 * arriving(h - 1, d) + c]
        dst = buf.at[2 * arriving(h, d) + c]
        at_row = 32 * half + 16 * i
        k = 4 * (h - 1) + 2 * d + i
        return remote(
            rows(src, at_row), rows(dst, at_row), ring_s.at[w, k], ring_r.at[w, k],
            same(1 if d == 0 else 7),
        )

    def side_copy(w, s, i):
        there = rows(full(w).at[2 * s + c], 32 * half + 16 * i)
        return pltpu.make_async_remote_copy(
            src_ref=there, dst_ref=there, send_sem=side_s.at[w, 2 * s + i],
            recv_sem=side_r.at[w, 2 * s + i],
            device_id={"doc": across[i]}, device_id_type=MESH,
        )

    def par_copy(w, s, j):
        if s == 0:
            src, dst = own[w], full(w).at[c]
        else:
            at_row = 32 * half + 16 * j if j < 2 else 32 * (1 - half) + 16 * (j - 2)
            src = dst = rows(full(w).at[2 * s + c], at_row)
        return remote(src, dst, par_s.at[w, 4 * s + j], par_r.at[w, 4 * s + j], partner)

    def own_copy(w):
        return pltpu.make_async_copy(own[w], full(w).at[c], own_s.at[w])

    def chunks(h):
        return [(d, i) for i in (0, 1) for d in (0, 1) if h < 4 or i == d]

    def launch(w):
        for d, i in chunks(1):
            ring_copy(w, 1, d, i).start()
        par_copy(w, 0, 0).start()
        own_copy(w).start()

    def hop(w, h):
        for d, i in chunks(h):
            ring_copy(w, h, d, i).wait_recv()
            if h < 4 and (d, i) in chunks(h + 1):
                ring_copy(w, h + 1, d, i).start()
            side_copy(w, arriving(h, d), i).start()
            par_copy(w, arriving(h, d), i).start()

    def lag(w, h):
        for d, i in chunks(h):
            side_copy(w, arriving(h, d), i).wait_recv()
            par_copy(w, arriving(h, d), 2 + i).start()

    def have(w, s):
        if s == 0:
            own_copy(w).wait()
            par_copy(w, 0, 0).wait_recv()
        else:
            for j in range(4):
                par_copy(w, s, j).wait_recv()

    def settle(w):
        for s in range(8):
            have(w, s)

    launch(0)
    tok_copy = remote(tok, tokh, tok_s, tok_r, far)
    tok_copy.start()

    xn = norm(tok[...].astype(F32))
    for p in range(8):
        xr[slot_of(p)] = xn[:, 128 * p : 128 * p + 128]

    row = lax.broadcasted_iota(jnp.int32, (128, 640), 0)
    col = lax.broadcasted_iota(jnp.int32, (128, 640), 1)
    for b in range(2):
        pos = me * 256 - 256 + 128 * b + col
        ok = (col >= row) & (col < row + 512) & (pos >= 0) & (pos < 4096)
        bias[b] = jnp.where(ok, 0.0, -1e30).astype(F32)

    def qkv_group(g):
        mine = jnp.concatenate([xr[2 * g], xr[2 * g + 1]], axis=1)
        both = jnp.concatenate(
            [mine, jnp.concatenate([xh[2 * g], xh[2 * g + 1]], axis=1)], axis=0
        )

        def tile_q(n, _):
            cols = pl.ds(pl.multiple_of(n * 512, 512), 512)
            part = nn(mine, wq[4 * g : 4 * g + 4, :, cols].reshape(256, 512))
            acc[n] = part if g == 0 else acc[n] + part
            return 0

        def tile_kv(n, _):
            cols = pl.ds(pl.multiple_of(1024 + n * 512, 512), 512)
            part = nn(both, wq[4 * g : 4 * g + 4, :, cols].reshape(256, 512))
            acch[n] = part if g == 0 else acch[n] + part
            return 0

        lax.fori_loop(0, 4, tile_kv, 0)
        lax.fori_loop(0, 2, tile_q, 0)

    hop(0, 1)
    hop(0, 2)
    lag(0, 1)
    tok_copy.wait_recv()
    xn = norm(tokh[...].astype(F32))
    for p in range(8):
        xh[slot_of(p)] = xn[:, 128 * p : 128 * p + 128]
    have(0, 0)
    have(0, 1)
    qkv_group(0)
    hop(0, 3)
    lag(0, 2)
    have(0, 2)
    have(0, 3)
    qkv_group(1)
    hop(0, 4)
    launch(1 + BO)
    launch(1 + CQ)
    launch(1 + TO)
    lag(0, 3)
    have(0, 4)
    have(0, 5)
    qkv_group(2)
    lag(0, 4)
    hop(1 + BO, 1)
    have(0, 6)
    have(0, 7)
    qkv_group(3)
    hop(1 + CQ, 1)
    hop(1 + TO, 1)

    far_rows = pl.ds(pl.multiple_of(512 * c, 256), 256)
    for n in range(4):
        block = acch[n].astype(BF16)
        for j in range(4):
            kv[(4 * n + j) % 8, n // 2, 256:512, :] = block[:256, 128 * j : 128 * j + 128]
            kv[(4 * n + j) % 8, n // 2, far_rows, :] = block[256:, 128 * j : 128 * j + 128]

    def halo(p):
        return remote(
            kv.at[p, :, pl.ds(256, 256), :], kv.at[p, :, far_rows, :],
            halo_s.at[p], halo_r.at[p], partner,
        )

    for n in range(2):
        block = acc[n].astype(BF16)
        for j in range(4):
            qb[4 * n + j] = block[:, 128 * j : 128 * j + 128]
    for p in range(8):
        halo(p).start()

    def event(*steps):
        def run():
            for step, w, *h in steps:
                step(1 + w, *h)
        return run

    hop(1 + BO, 2)
    lag(1 + BO, 1)
    launch(1 + CO)
    events = {
        0: event((hop, CQ, 2), (lag, CQ, 1)),
        1: event((hop, TO, 2), (lag, TO, 1)),
        2: event((hop, BO, 3), (lag, BO, 2)),
        3: event((hop, CQ, 3), (lag, CQ, 2)),
        4: event((hop, TO, 3), (lag, TO, 2)),
        5: event((hop, CO, 1)),
        6: event((hop, BO, 4), (lag, BO, 3)),
        7: event((hop, CQ, 4), (lag, CQ, 3), (lag, BO, 4)),
    }

    def attention(p, _):
        halo(p).wait_recv()
        slot = slot_of(p)
        even = lax.broadcasted_iota(jnp.int32, (128, 128), 1) < 64
        for b in range(2):
            q = qb[p, 128 * b : 128 * b + 128, :]
            zero = jnp.zeros_like(q)
            both = jnp.concatenate([jnp.where(even, q, zero), jnp.where(even, zero, q)], axis=0)
            s = nt(both, kv[p, 0, 128 * b : 128 * b + 640, :])
            s = (s.reshape(2, 128, 640) + bias[b][None]).reshape(256, 640)
            e = jnp.exp2((s - jnp.max(s, axis=1, keepdims=True)) * EXP_SCALE)
            total = jnp.sum(e, axis=1, keepdims=True)
            o = nn(e.astype(BF16), kv[p, 1, 128 * b : 128 * b + 640, :]) / total
            at[slot, 128 * b : 128 * b + 128, :] = jnp.where(even, o[:128], o[128:]).astype(BF16)
        for k, event in events.items():
            pl.when(p == k)(event)
        return 0

    lax.fori_loop(0, 8, attention, 0)

    def square(lhs8, w, put):
        lhs = jnp.concatenate([lhs8[s] for s in range(8)], axis=1)

        def tile(n, _):
            cols = pl.ds(pl.multiple_of(n * 256, 256), 256)
            put(n, cols, nn(lhs, w2[w, :, :, cols].reshape(1024, 256)))
            return 0

        lax.fori_loop(0, 4, tile, 0)

    settle(1 + BO)

    def put_lower(n, cols, o):
        lt[:, cols] = (tok[:, cols].astype(F32) + o).astype(BF16)

    square(at, BO, put_lower)

    def cast_copies(b, buf):
        mine = buf.at[me]
        sends = [remote(mine, mine, cast_s.at[b, 0], cast_r.at[b, 0], partner)]
        for r in range(1, 8):
            sends.append(remote(mine, mine, cast_s.at[b, r], cast_r.at[b, r], same(r)))
        return sends

    def fwd_copy(b, buf, r):
        there = buf.at[same(8 - r)]
        return remote(there, there, fwd_s.at[b, r], fwd_r.at[b, r], partner)

    def cast_start(b, buf):
        sends = cast_copies(b, buf)
        for r in (4, 3, 5, 2, 6, 1, 7, 0):
            sends[r].start()

    def cast_finish(b, buf):
        sends = cast_copies(b, buf)
        for r in NEAREST:
            sends[r].wait_recv()
            fwd_copy(b, buf, r).start()
        sends[0].wait_recv()
        for r in NEAREST:
            fwd_copy(b, buf, r).wait_recv()

    low = lt[...].astype(F32)
    pooled[me] = (jnp.sum(low.reshape(8, POOL, 1024), axis=1) * (1.0 / POOL)).astype(BF16)
    cast_start(0, pooled)
    hop(1 + TO, 4)
    lag(1 + TO, 3)
    hop(1 + CO, 2)
    lag(1 + CO, 1)
    lag(1 + CQ, 4)
    ln = norm(low)
    for p in range(8):
        xr[slot_of(p)] = ln[:, 128 * p : 128 * p + 128]
    lag(1 + TO, 4)
    hop(1 + CO, 3)
    lag(1 + CO, 2)
    cast_finish(0, pooled)

    units = pooled[...].astype(F32).reshape(128, 1024)
    for copy in unit_copies:
        copy.wait()
    un = norm(units)
    tq = nt(un, tqt[0]).astype(BF16)
    tk = nt(un, tqt[1]).astype(BF16)
    tvt = nt(tqt[2], un).astype(BF16)
    st = nt(tk, tq)
    e = jnp.exp2((st - jnp.max(st, axis=0, keepdims=True)) * EXP_SCALE)
    tat[me] = (nn(tvt, e.astype(BF16)) / jnp.sum(e, axis=0, keepdims=True)).astype(BF16)
    cast_start(1, tat)
    hop(1 + CO, 4)
    lag(1 + CO, 3)
    settle(1 + CQ)

    def put_query(n, cols, o):
        o = o.astype(BF16)
        cq[2 * n] = o[:, :128]
        cq[2 * n + 1] = o[:, 128:]

    square(xr, CQ, put_query)
    lag(1 + CO, 4)
    cast_finish(1, tat)
    settle(1 + TO)

    chips = []
    for s in range(8):
        off = (s + 1) // 2 * (1 - 2 * (s % 2))
        base = 2 * ((z + 8 + off) % 8)
        chips.append(tat[pl.ds(base, 2)].reshape(128, 128).T)
    ta = jnp.concatenate(chips, axis=1)
    units = units + nn(ta, w2[TO].reshape(1024, 1024))
    up = norm(units.astype(BF16).astype(F32))
    ckv[me, 0] = nt(ckt[0], up).astype(BF16)
    ckv[me, 1] = nt(ckt[1], up).astype(BF16)
    cast_start(2, ckv)
    settle(1 + CO)
    cast_finish(2, ckv)

    def cross(p, _):
        q = cq[p]
        even = lax.broadcasted_iota(jnp.int32, (256, 128), 1) < 64
        zero = jnp.zeros_like(q)
        both = jnp.concatenate([jnp.where(even, q, zero), jnp.where(even, zero, q)], axis=0)
        s = nn(both, ckv[pl.ds(2 * p, 2), 0].reshape(128, 128))
        e = jnp.exp2((s - jnp.max(s, axis=1, keepdims=True)) * EXP_SCALE)
        total = jnp.sum(e, axis=1, keepdims=True)
        o = nt(e.astype(BF16), ckv[pl.ds(2 * p, 2), 1].reshape(128, 128)) / total
        at[slot_of(p)] = jnp.where(even, o[:256], o[256:]).astype(BF16)
        return 0

    lax.fori_loop(0, 8, cross, 0)

    def put_out(n, cols, o):
        out[:, cols] = (lt[:, cols].astype(F32) + o).astype(BF16)

    square(at, CO, put_out)

    for w in range(5):
        par_copy(w, 0, 0).wait_send()
        for h in range(1, 5):
            for d, i in chunks(h):
                ring_copy(w, h, d, i).wait_send()
                side_copy(w, arriving(h, d), i).wait_send()
                par_copy(w, arriving(h, d), i).wait_send()
                par_copy(w, arriving(h, d), 2 + i).wait_send()
    tok_copy.wait_send()
    for p in range(8):
        halo(p).wait_send()
    for b, buf in enumerate((pooled, tat, ckv)):
        for copy in cast_copies(b, buf):
            copy.wait_send()
        for r in range(1, 8):
            fwd_copy(b, buf, r).wait_send()


def local(tokens, bottom_qkv, bottom_out, top_qkv, top_out, cross_query, cross_kv, cross_out):
    tqt = top_qkv.transpose(1, 2, 0)
    ckt = cross_kv.transpose(1, 2, 0)
    dma = pltpu.SemaphoreType.DMA
    return pl.pallas_call(
        kernel,
        out_shape=jax.ShapeDtypeStruct((256, 1024), BF16),
        in_specs=[pl.BlockSpec(memory_space=pltpu.VMEM)] + [pl.BlockSpec(memory_space=pl.ANY)] * 7,
        out_specs=pl.BlockSpec(memory_space=pltpu.VMEM),
        scratch_shapes=[
            pltpu.VMEM((16, 64, 3072), BF16),
            pltpu.VMEM((4, 16, 64, 1024), BF16),
            pltpu.VMEM((8, 256, 128), BF16),
            pltpu.VMEM((2, 256, 512), F32),
            pltpu.VMEM((8, 256, 128), BF16),
            pltpu.VMEM((8, 2, 768, 128), BF16),
            pltpu.VMEM((2, 128, 640), F32),
            pltpu.VMEM((8, 256, 128), BF16),
            pltpu.VMEM((256, 1024), BF16),
            pltpu.VMEM((16, 8, 1024), BF16),
            pltpu.VMEM((16, 64, 128), BF16),
            pltpu.VMEM((16, 2, 64, 128), BF16),
            pltpu.VMEM((8, 256, 128), BF16),
            pltpu.VMEM((256, 1024), BF16),
            pltpu.VMEM((8, 256, 128), BF16),
            pltpu.VMEM((4, 512, 512), F32),
            dma((5, 16)), dma((5, 16)), dma((5, 32)), dma((5, 32)), dma((5,)),
            dma((8,)), dma((8,)),
            dma((3, 8)), dma((3, 8)), dma((3, 8)), dma((3, 8)),
            dma((5, 16)), dma((5, 16)), dma, dma,
            pltpu.VMEM((3, 64, 1024), BF16), pltpu.VMEM((2, 64, 1024), BF16), dma((2,)),
        ],
        compiler_params=pltpu.CompilerParams(
            collective_id=0, has_side_effects=True, vmem_limit_bytes=60 * 1024 * 1024
        ),
        name="layer",
    )(tokens, bottom_qkv, bottom_out, cross_query, top_out, cross_out, tqt, ckt)


def solution(mesh):
    in_specs = (
        P(("doc", "seq"), None),
        P("seq", None),
        P("seq", None),
        P(None, None, "seq"),
        P("seq", None),
        P("seq", None),
        P(None, None, "seq"),
        P("seq", None),
    )
    out_specs = P(("doc", "seq"), None)
    return jax.shard_map(local, mesh=mesh, in_specs=in_specs, out_specs=out_specs, check_vma=False)
```

```python
import math

import jax
import jax.numpy as jnp
from jax import lax
from jax.experimental import pallas as pl
from jax.experimental.pallas import tpu as pltpu
from jax.sharding import PartitionSpec as P

POOL = 32
EPS = 1e-06
F32 = jnp.float32
BF16 = jnp.bfloat16
EXP_SCALE = math.log2(math.e) / 8.0
MESH = pl.DeviceIdType.MESH
BO, CQ, TO, CO = 0, 1, 2, 3
NEAREST = (1, 7, 2, 6, 3, 5, 4)


def nt(a, b):
    return lax.dot_general(a, b, (((1,), (1,)), ((), ())), preferred_element_type=F32)


def nn(a, b):
    return jnp.dot(a, b, preferred_element_type=F32)


def norm(v):
    return (v * lax.rsqrt(jnp.mean(v * v, axis=-1, keepdims=True) + EPS)).astype(BF16)


def kernel(
    tok_hbm, w_qkv, w_bo, w_cq, w_to, w_co, tq_hbm, ck_hbm, out,
    wq, w2, xr, acc, qb, kv, bias, at, lt, pooled, tat, ckv, cq, tokh, xh, acch,
    ring_s, ring_r, par_s, par_r, own_s, halo_s, halo_r, cast_s, cast_r, fwd_s, fwd_r,
    side_s, side_r, tok_s, tok_r, tqt, ckt, unit_s, tok, out_v, out_s,
):
    me = lax.axis_index("seq")
    z, c = me // 2, me % 2
    partner = 2 * z + 1 - c

    def same(r):
        return 2 * ((z + r) % 8) + c

    doc = lax.axis_index("doc")
    x, y = doc % 4, doc // 4
    half = (x + y) % 2
    across = (4 * y + x + 1 - 2 * (x % 2), 4 * (y + 1 - 2 * (y % 2)) + x)
    far = (me + 16 + (2 * c - 1)) % 16

    def slot_of(p):
        d = (p + 8 - z) % 8
        up = d // 4
        return (1 - up) * 2 * d + up * (15 - 2 * d)

    def remote(src, dst, s, r, to):
        return pltpu.make_async_remote_copy(
            src_ref=src, dst_ref=dst, send_sem=s, recv_sem=r,
            device_id={"seq": to}, device_id_type=MESH,
        )

    tok_in = pltpu.make_async_copy(tok_hbm, tok, unit_s.at[2])
    tok_in.start()
    unit_copies = (
        pltpu.make_async_copy(tq_hbm, tqt, unit_s.at[0]),
        pltpu.make_async_copy(ck_hbm, ckt, unit_s.at[1]),
    )
    for copy in unit_copies:
        copy.start()
    barrier = pltpu.get_barrier_semaphore()
    for peer in [same(r) for r in range(1, 8)] + [partner, far]:
        pl.semaphore_signal(barrier, inc=1, device_id={"seq": peer}, device_id_type=MESH)
    for peer in across:
        pl.semaphore_signal(barrier, inc=1, device_id={"doc": peer}, device_id_type=MESH)
    pl.semaphore_wait(barrier, 11)

    own = [w_qkv, w_bo, w_cq, w_to, w_co]

    def full(w):
        return wq if w == 0 else w2.at[w - 1]

    def arriving(h, d):
        return 7 if h == 4 else 2 * h - 1 + d

    def rows(buf, start):
        return buf.at[pl.ds(pl.multiple_of(start, 16), 16)]

    def ring_copy(w, h, d, i):
        buf = full(w)
        src = own[w] if h == 1 else buf.at[2 * arriving(h - 1, d) + c]
        dst = buf.at[2 * arriving(h, d) + c]
        at_row = 32 * half + 16 * i
        k = 4 * (h - 1) + 2 * d + i
        return remote(
            rows(src, at_row), rows(dst, at_row), ring_s.at[w, k], ring_r.at[w, k],
            same(1 if d == 0 else 7),
        )

    def side_copy(w, s, i):
        there = rows(full(w).at[2 * s + c], 32 * half + 16 * i)
        return pltpu.make_async_remote_copy(
            src_ref=there, dst_ref=there, send_sem=side_s.at[w, 2 * s + i],
            recv_sem=side_r.at[w, 2 * s + i],
            device_id={"doc": across[i]}, device_id_type=MESH,
        )

    def par_copy(w, s, j):
        if s == 0:
            src, dst = own[w], full(w).at[c]
        else:
            at_row = 32 * half + 16 * j if j < 2 else 32 * (1 - half) + 16 * (j - 2)
            src = dst = rows(full(w).at[2 * s + c], at_row)
        return remote(src, dst, par_s.at[w, 4 * s + j], par_r.at[w, 4 * s + j], partner)

    def own_copy(w):
        return pltpu.make_async_copy(own[w], full(w).at[c], own_s.at[w])

    def chunks(h):
        return [(d, i) for i in (0, 1) for d in (0, 1) if h < 4 or i == d]

    def launch(w):
        for d, i in chunks(1):
            ring_copy(w, 1, d, i).start()
        par_copy(w, 0, 0).start()
        own_copy(w).start()

    def hop(w, h):
        for d, i in chunks(h):
            ring_copy(w, h, d, i).wait_recv()
            if h < 4 and (d, i) in chunks(h + 1):
                ring_copy(w, h + 1, d, i).start()
            side_copy(w, arriving(h, d), i).start()
            par_copy(w, arriving(h, d), i).start()

    def lag(w, h):
        for d, i in chunks(h):
            side_copy(w, arriving(h, d), i).wait_recv()
            par_copy(w, arriving(h, d), 2 + i).start()

    def have(w, s):
        if s == 0:
            own_copy(w).wait()
            par_copy(w, 0, 0).wait_recv()
        else:
            for j in range(4):
                par_copy(w, s, j).wait_recv()

    def settle(w):
        for s in range(8):
            have(w, s)

    launch(0)
    tok_copy = remote(tok_hbm, tokh, tok_s, tok_r, far)
    tok_copy.start()

    tok_in.wait()
    xn = norm(tok[...].astype(F32))
    for p in range(8):
        xr[slot_of(p)] = xn[:, 128 * p : 128 * p + 128]

    row = lax.broadcasted_iota(jnp.int32, (128, 640), 0)
    col = lax.broadcasted_iota(jnp.int32, (128, 640), 1)
    for b in range(2):
        pos = me * 256 - 256 + 128 * b + col
        ok = (col >= row) & (col < row + 512) & (pos >= 0) & (pos < 4096)
        bias[b] = jnp.where(ok, 0.0, -1e30).astype(F32)

    def qkv_group(g):
        mine = jnp.concatenate([xr[2 * g], xr[2 * g + 1]], axis=1)
        both = jnp.concatenate(
            [mine, jnp.concatenate([xh[2 * g], xh[2 * g + 1]], axis=1)], axis=0
        )

        def tile_q(n, _):
            cols = pl.ds(pl.multiple_of(n * 512, 512), 512)
            part = nn(mine, wq[4 * g : 4 * g + 4, :, cols].reshape(256, 512))
            acc[n] = part if g == 0 else acc[n] + part
            return 0

        def tile_kv(n, _):
            cols = pl.ds(pl.multiple_of(1024 + n * 512, 512), 512)
            part = nn(both, wq[4 * g : 4 * g + 4, :, cols].reshape(256, 512))
            acch[n] = part if g == 0 else acch[n] + part
            return 0

        lax.fori_loop(0, 4, tile_kv, 0)
        lax.fori_loop(0, 2, tile_q, 0)

    hop(0, 1)
    hop(0, 2)
    lag(0, 1)
    tok_copy.wait_recv()
    xn = norm(tokh[...].astype(F32))
    for p in range(8):
        xh[slot_of(p)] = xn[:, 128 * p : 128 * p + 128]
    have(0, 0)
    have(0, 1)
    qkv_group(0)
    hop(0, 3)
    lag(0, 2)
    have(0, 2)
    have(0, 3)
    qkv_group(1)
    hop(0, 4)
    launch(1 + BO)
    launch(1 + CQ)
    launch(1 + TO)
    lag(0, 3)
    have(0, 4)
    have(0, 5)
    qkv_group(2)
    lag(0, 4)
    hop(1 + BO, 1)
    have(0, 6)
    have(0, 7)
    qkv_group(3)
    hop(1 + CQ, 1)
    hop(1 + TO, 1)

    far_rows = pl.ds(pl.multiple_of(512 * c, 256), 256)
    for n in range(4):
        block = acch[n].astype(BF16)
        for j in range(4):
            kv[(4 * n + j) % 8, n // 2, 256:512, :] = block[:256, 128 * j : 128 * j + 128]
            kv[(4 * n + j) % 8, n // 2, far_rows, :] = block[256:, 128 * j : 128 * j + 128]

    def halo(p):
        return remote(
            kv.at[p, :, pl.ds(256, 256), :], kv.at[p, :, far_rows, :],
            halo_s.at[p], halo_r.at[p], partner,
        )

    for n in range(2):
        block = acc[n].astype(BF16)
        for j in range(4):
            qb[4 * n + j] = block[:, 128 * j : 128 * j + 128]
    for p in range(8):
        halo(p).start()

    def event(*steps):
        def run():
            for step, w, *h in steps:
                step(1 + w, *h)
        return run

    hop(1 + BO, 2)
    lag(1 + BO, 1)
    launch(1 + CO)
    events = {
        0: event((hop, CQ, 2), (lag, CQ, 1)),
        1: event((hop, TO, 2), (lag, TO, 1)),
        2: event((hop, BO, 3), (lag, BO, 2)),
        3: event((hop, CQ, 3), (lag, CQ, 2)),
        4: event((hop, TO, 3), (lag, TO, 2)),
        5: event((hop, CO, 1)),
        6: event((hop, BO, 4), (lag, BO, 3)),
        7: event((hop, CQ, 4), (lag, CQ, 3), (lag, BO, 4)),
    }

    def attention(p, _):
        halo(p).wait_recv()
        slot = slot_of(p)
        even = lax.broadcasted_iota(jnp.int32, (128, 128), 1) < 64
        for b in range(2):
            q = qb[p, 128 * b : 128 * b + 128, :]
            zero = jnp.zeros_like(q)
            both = jnp.concatenate([jnp.where(even, q, zero), jnp.where(even, zero, q)], axis=0)
            s = nt(both, kv[p, 0, 128 * b : 128 * b + 640, :])
            s = (s.reshape(2, 128, 640) + bias[b][None]).reshape(256, 640)
            e = jnp.exp2((s - jnp.max(s, axis=1, keepdims=True)) * EXP_SCALE)
            total = jnp.sum(e, axis=1, keepdims=True)
            o = nn(e.astype(BF16), kv[p, 1, 128 * b : 128 * b + 640, :]) / total
            at[slot, 128 * b : 128 * b + 128, :] = jnp.where(even, o[:128], o[128:]).astype(BF16)
        for k, event in events.items():
            pl.when(p == k)(event)
        return 0

    lax.fori_loop(0, 8, attention, 0)

    def square(lhs8, w, put):
        lhs = jnp.concatenate([lhs8[s] for s in range(8)], axis=1)

        def tile(n, _):
            cols = pl.ds(pl.multiple_of(n * 256, 256), 256)
            put(n, cols, nn(lhs, w2[w, :, :, cols].reshape(1024, 256)))
            return 0

        lax.fori_loop(0, 4, tile, 0)

    settle(1 + BO)

    def put_lower(n, cols, o):
        lt[:, cols] = (tok[:, cols].astype(F32) + o).astype(BF16)

    square(at, BO, put_lower)

    def cast_copies(b, buf):
        mine = buf.at[me]
        sends = [remote(mine, mine, cast_s.at[b, 0], cast_r.at[b, 0], partner)]
        for r in range(1, 8):
            sends.append(remote(mine, mine, cast_s.at[b, r], cast_r.at[b, r], same(r)))
        return sends

    def fwd_copy(b, buf, r):
        there = buf.at[same(8 - r)]
        return remote(there, there, fwd_s.at[b, r], fwd_r.at[b, r], partner)

    def cast_start(b, buf):
        sends = cast_copies(b, buf)
        for r in (4, 3, 5, 2, 6, 1, 7, 0):
            sends[r].start()

    def cast_finish(b, buf):
        sends = cast_copies(b, buf)
        for r in NEAREST:
            sends[r].wait_recv()
            fwd_copy(b, buf, r).start()
        sends[0].wait_recv()
        for r in NEAREST:
            fwd_copy(b, buf, r).wait_recv()

    low = lt[...].astype(F32)
    pooled[me] = (jnp.sum(low.reshape(8, POOL, 1024), axis=1) * (1.0 / POOL)).astype(BF16)
    cast_start(0, pooled)
    hop(1 + TO, 4)
    lag(1 + TO, 3)
    hop(1 + CO, 2)
    lag(1 + CO, 1)
    lag(1 + CQ, 4)
    ln = norm(low)
    for p in range(8):
        xr[slot_of(p)] = ln[:, 128 * p : 128 * p + 128]
    lag(1 + TO, 4)
    hop(1 + CO, 3)
    lag(1 + CO, 2)
    cast_finish(0, pooled)

    units = pooled[...].astype(F32).reshape(128, 1024)
    for copy in unit_copies:
        copy.wait()
    un = norm(units)
    tq = nt(un, tqt[0]).astype(BF16)
    tk = nt(un, tqt[1]).astype(BF16)
    tvt = nt(tqt[2], un).astype(BF16)
    st = nt(tk, tq)
    e = jnp.exp2((st - jnp.max(st, axis=0, keepdims=True)) * EXP_SCALE)
    tat[me] = (nn(tvt, e.astype(BF16)) / jnp.sum(e, axis=0, keepdims=True)).astype(BF16)
    cast_start(1, tat)
    hop(1 + CO, 4)
    lag(1 + CO, 3)
    settle(1 + CQ)

    def put_query(n, cols, o):
        o = o.astype(BF16)
        cq[2 * n] = o[:, :128]
        cq[2 * n + 1] = o[:, 128:]

    square(xr, CQ, put_query)
    lag(1 + CO, 4)
    cast_finish(1, tat)
    settle(1 + TO)

    chips = []
    for s in range(8):
        off = (s + 1) // 2 * (1 - 2 * (s % 2))
        base = 2 * ((z + 8 + off) % 8)
        chips.append(tat[pl.ds(base, 2)].reshape(128, 128).T)
    ta = jnp.concatenate(chips, axis=1)
    units = units + nn(ta, w2[TO].reshape(1024, 1024))
    up = norm(units.astype(BF16).astype(F32))
    ckv[me, 0] = nt(ckt[0], up).astype(BF16)
    ckv[me, 1] = nt(ckt[1], up).astype(BF16)
    cast_start(2, ckv)
    settle(1 + CO)
    cast_finish(2, ckv)

    def cross(p, _):
        q = cq[p]
        even = lax.broadcasted_iota(jnp.int32, (256, 128), 1) < 64
        zero = jnp.zeros_like(q)
        both = jnp.concatenate([jnp.where(even, q, zero), jnp.where(even, zero, q)], axis=0)
        s = nn(both, ckv[pl.ds(2 * p, 2), 0].reshape(128, 128))
        e = jnp.exp2((s - jnp.max(s, axis=1, keepdims=True)) * EXP_SCALE)
        total = jnp.sum(e, axis=1, keepdims=True)
        o = nt(e.astype(BF16), ckv[pl.ds(2 * p, 2), 1].reshape(128, 128)) / total
        at[slot_of(p)] = jnp.where(even, o[:256], o[256:]).astype(BF16)
        return 0

    lax.fori_loop(0, 8, cross, 0)

    def put_out(n, cols, o):
        out_v[n] = (lt[:, cols].astype(F32) + o).astype(BF16)
        pltpu.make_async_copy(out_v.at[n], out.at[:, cols], out_s.at[n]).start()

    square(at, CO, put_out)

    for n in range(4):
        cols = pl.ds(256 * n, 256)
        pltpu.make_async_copy(out_v.at[n], out.at[:, cols], out_s.at[n]).wait()
    for w in range(5):
        par_copy(w, 0, 0).wait_send()
        for h in range(1, 5):
            for d, i in chunks(h):
                ring_copy(w, h, d, i).wait_send()
                side_copy(w, arriving(h, d), i).wait_send()
                par_copy(w, arriving(h, d), i).wait_send()
                par_copy(w, arriving(h, d), 2 + i).wait_send()
    tok_copy.wait_send()
    for p in range(8):
        halo(p).wait_send()
    for b, buf in enumerate((pooled, tat, ckv)):
        for copy in cast_copies(b, buf):
            copy.wait_send()
        for r in range(1, 8):
            fwd_copy(b, buf, r).wait_send()


def local(tokens, bottom_qkv, bottom_out, top_qkv, top_out, cross_query, cross_kv, cross_out):
    tqt = top_qkv.transpose(1, 2, 0)
    ckt = cross_kv.transpose(1, 2, 0)
    dma = pltpu.SemaphoreType.DMA
    return pl.pallas_call(
        kernel,
        out_shape=jax.ShapeDtypeStruct((256, 1024), BF16),
        in_specs=[pl.BlockSpec(memory_space=pl.ANY)] * 8,
        out_specs=pl.BlockSpec(memory_space=pl.ANY),
        scratch_shapes=[
            pltpu.VMEM((16, 64, 3072), BF16),
            pltpu.VMEM((4, 16, 64, 1024), BF16),
            pltpu.VMEM((8, 256, 128), BF16),
            pltpu.VMEM((2, 256, 512), F32),
            pltpu.VMEM((8, 256, 128), BF16),
            pltpu.VMEM((8, 2, 768, 128), BF16),
            pltpu.VMEM((2, 128, 640), F32),
            pltpu.VMEM((8, 256, 128), BF16),
            pltpu.VMEM((256, 1024), BF16),
            pltpu.VMEM((16, 8, 1024), BF16),
            pltpu.VMEM((16, 64, 128), BF16),
            pltpu.VMEM((16, 2, 64, 128), BF16),
            pltpu.VMEM((8, 256, 128), BF16),
            pltpu.VMEM((256, 1024), BF16),
            pltpu.VMEM((8, 256, 128), BF16),
            pltpu.VMEM((4, 512, 512), F32),
            dma((5, 16)), dma((5, 16)), dma((5, 32)), dma((5, 32)), dma((5,)),
            dma((8,)), dma((8,)),
            dma((3, 8)), dma((3, 8)), dma((3, 8)), dma((3, 8)),
            dma((5, 16)), dma((5, 16)), dma, dma,
            pltpu.VMEM((3, 64, 1024), BF16), pltpu.VMEM((2, 64, 1024), BF16), dma((3,)),
            pltpu.VMEM((256, 1024), BF16), pltpu.VMEM((4, 256, 256), BF16), dma((4,)),
        ],
        compiler_params=pltpu.CompilerParams(
            collective_id=0, has_side_effects=True, vmem_limit_bytes=60 * 1024 * 1024
        ),
        name="layer",
    )(tokens, bottom_qkv, bottom_out, cross_query, top_out, cross_out, tqt, ckt)


def solution(mesh):
    in_specs = (
        P(("doc", "seq"), None),
        P("seq", None),
        P("seq", None),
        P(None, None, "seq"),
        P("seq", None),
        P("seq", None),
        P(None, None, "seq"),
        P("seq", None),
    )
    out_specs = P(("doc", "seq"), None)
    return jax.shard_map(local, mesh=mesh, in_specs=in_specs, out_specs=out_specs, check_vma=False)
```
